32 devices in a mesh: seq: 16 (over z, x, core), mp: 2 (over y).
Axes of the slice: x: 2, y: 2, z: 4, core: 2. Of those that a mesh axis runs over, the one named last changes fastest.
Arguments:
- queries: bfloat16 [4096, 5120], P('seq', 'mp'), may hold values from -40 to 40
- keys: bfloat16 [4096, 1024], P('seq', 'mp'), may hold values from -8 to 8
- values: bfloat16 [4096, 1024], P('seq', 'mp'), may hold values from -6 to 6
- segment_ids: int32 [4096], P('seq'), may hold values from 0 to 3, never falling along the last dimension, each value on 1 to 2048 neighbouring positions
- page_slots: int32 [256], P('seq'), may hold values from 0 to 255, as said below
Outputs:
- context: bfloat16 [4096, 5120], P('seq', 'mp')
- cache: bfloat16 [256, 16, 2048], P('seq', 'mp')
The draws below stay inside these ranges and needn't reach their ends.
Inputs may be any that keep to these rules, and one draw needn't show every extreme that they name: `page_slots`: the pages of the 256 tokens on one index of seq are mapped one to one onto that index's own 16 cache rows.
All inputs are finite; a program needn't handle non-finite values.
Results may differ from the reference program's by a relative error of at most 0.0041.
Values may be sent and summed in bfloat16 or wider, within the bound.
A program may use at most 64 MiB of HBM per device.

```python
import math
import jax
import jax.numpy as jnp
import numpy as np
from jax import lax

QH = 40
KVH = 8
HD = 128
TOK_DEV = 256
LMAX = 2048
PAGE = 16
TOKENS = 4096
SEGS = 4
PAGE_DEV = 16
PAGES = 256


def joint_draw(key):
    first, second = jax.random.split(jax.random.fold_in(key, 7), 2)
    key_vecs = jnp.clip(jax.random.normal(first, (TOKENS, KVH, HD), jnp.float32), -6.0, 6.0)
    query_vecs = 0.5 * jnp.clip(jax.random.normal(second, (TOKENS, QH, HD), jnp.float32), -6.0, 6.0)
    return (query_vecs.reshape(TOKENS, QH * HD), key_vecs.reshape(TOKENS, KVH * HD))


def draw_queries(key, part):
    return joint_draw(key)[0].astype(jnp.bfloat16)


def draw_keys(key, part):
    return joint_draw(key)[1].astype(jnp.bfloat16)


def draw_page_slots(key, part):
    blocks = PAGES // PAGE_DEV
    subkeys = jax.random.split(jax.random.fold_in(key, 11), blocks)
    orders = jax.vmap(lambda sub: jax.random.permutation(sub, PAGE_DEV))(subkeys)
    offsets = jnp.arange(blocks, dtype=jnp.int32)[:, None] * PAGE_DEV
    return (orders.astype(jnp.int32) + offsets).reshape(PAGES)


def shard_levels(stream_key, extent, cuts, least, largest):
    def one(dim, parts):
        heights = jax.random.uniform(jax.random.fold_in(jax.random.fold_in(stream_key, 6), dim), (parts,), jnp.float32, least / len(cuts), largest / len(cuts))
        return jnp.repeat(jnp.exp(heights), extent[dim] // parts).reshape((-1,) + (1,) * (len(extent) - dim - 1))

    factor_of = one(*cuts[0])
    for cut in cuts[1:]:
        factor_of = factor_of * one(*cut)
    return factor_of


def profile(count, total, reach, slope):
    portions = [(1 << 20) // math.isqrt(rank ** slope) + 1 for rank in range(2, count + 1)]
    spare, counts = total - reach - (count - 1), [1] * (count - 1)
    while spare > 0:
        movable = [i for i in range(count - 1) if counts[i] < reach]
        pool, remaining = sum([portions[i] for i in movable]), spare
        for i in movable:
            extra = min(reach - counts[i], max(1, remaining * portions[i] // pool), spare)
            counts[i] = counts[i] + extra
            spare = spare - extra
    return np.array([reach] + counts)


def ragged_sizes(key, number_of, total, most, skew):
    if number_of == 2:
        one = jax.random.randint(key, (), max(1, total - most), min(most, total - 1) + 1)
        return jnp.stack([one, total - one])
    lengths = jnp.asarray(profile(number_of, total, most, skew), jnp.int32)
    pairs = (number_of - 1) // 2
    giver, sink = lengths[1:1 + 2 * pairs:2], lengths[2:2 + 2 * pairs:2]
    room = jnp.minimum(giver - 1, most - sink)
    passed = jax.random.randint(jax.random.fold_in(key, 1), (pairs,), 0, 1 << 20) % (room + 1)
    lengths = lengths.at[1:1 + 2 * pairs:2].set(giver - passed).at[2:2 + 2 * pairs:2].set(sink + passed)
    return lengths[jax.random.permutation(jax.random.fold_in(key, 2), number_of)]


def bell_draw(rng, dims, scale, most, cuts=(), kind=jnp.bfloat16):
    entries = jax.random.normal(rng, dims, jnp.float32) * scale
    if len(cuts) > 0:
        entries = shard_levels(rng, dims, cuts, -0.22, 0.18) * entries
    return jnp.clip(entries, min=-most, max=most).astype(kind)


def setup_inputs(seed: int = 0) -> dict:
    splits = jax.random.split(jax.random.key(seed), 6)
    queries = draw_queries(jax.random.fold_in(splits[5], 71), 0)
    keys = draw_keys(jax.random.fold_in(splits[5], 71), 0)
    values = bell_draw(splits[2], (TOKENS, KVH * HD), 1.0, 6.0, ((0, 16), (1, 2)))
    segment_ids = jnp.searchsorted(jnp.cumsum(ragged_sizes(splits[3], SEGS, TOKENS, LMAX, 2)), jnp.arange(TOKENS), side="right").astype(jnp.int32)
    page_slots = draw_page_slots(jax.random.fold_in(splits[5], 71), 0)
    return dict(queries=queries, keys=keys, values=values, segment_ids=segment_ids, page_slots=page_slots)


def reference(queries, keys, values, segment_ids, page_slots):
    group = QH // KVH
    width = LMAX + TOK_DEV
    scale = 1.0 / (HD ** 0.5)
    rows = jnp.arange(TOK_DEV, dtype=jnp.int32)
    cols = jnp.arange(width, dtype=jnp.int32)

    def one_block(index):
        start = (index * TOK_DEV).astype(jnp.int32)
        lower = jnp.maximum(start - LMAX, 0).astype(jnp.int32)
        query_block = lax.dynamic_slice_in_dim(queries, start, TOK_DEV, 0).astype(jnp.float32)
        query_block = query_block.reshape(TOK_DEV, KVH, group, HD)
        key_block = lax.dynamic_slice_in_dim(keys, lower, width, 0).astype(jnp.float32).reshape(width, KVH, HD)
        value_block = lax.dynamic_slice_in_dim(values, lower, width, 0).astype(jnp.float32).reshape(width, KVH, HD)
        query_seg = lax.dynamic_slice_in_dim(segment_ids, start, TOK_DEV, 0)
        key_seg = lax.dynamic_slice_in_dim(segment_ids, lower, width, 0)
        query_pos = start + rows
        key_pos = lower + cols
        allowed = (key_seg[None, :] == query_seg[:, None]) & (key_pos[None, :] <= query_pos[:, None])
        score = jnp.einsum("qkgd,pkd->kgqp", query_block, key_block, precision=lax.Precision.HIGHEST) * scale
        score = jnp.where(allowed, score, -1e30)
        top = jnp.max(score, axis=-1, keepdims=True)
        expo = jnp.where(allowed, jnp.exp(score - top), 0.0)
        total = jnp.sum(expo, axis=-1)
        rounded = lax.optimization_barrier(expo.astype(jnp.bfloat16)).astype(jnp.float32)
        out = jnp.einsum("kgqp,pkd->kgqd", rounded, value_block, precision=lax.Precision.HIGHEST)
        out = out / total[..., None]
        out = jnp.transpose(out, (2, 0, 1, 3))
        return out.reshape(TOK_DEV, QH * HD).astype(jnp.bfloat16)

    blocks = lax.map(one_block, jnp.arange(TOKENS // TOK_DEV, dtype=jnp.int32))
    context = blocks.reshape(TOKENS, QH * HD)
    pages = jnp.stack([keys, values], axis=1).reshape(PAGES, PAGE, 2 * KVH * HD)
    cache = jnp.zeros((PAGES, PAGE, 2 * KVH * HD), jnp.bfloat16).at[page_slots].set(pages)
    return context, cache
```

```python
import functools
import math

import jax
import jax.numpy as jnp
from jax import lax
from jax.experimental import pallas as pl
from jax.experimental.pallas import tpu as pltpu
from jax.sharding import PartitionSpec as P

HD = 128
LMAX = 2048
PLANE = 4
LEVELS = 3
BIG = 2.0**30
HEAD = 2
SEG_ROWS = 16
EXP_SCALE = math.log2(math.e) / math.sqrt(HD)
NT = (((1,), (1,)), ((), ()))
NN = (((1,), (0,)), ((), ()))


def kernel(
    n,
    heads,
    group,
    q_hbm,
    k_hbm,
    v_hbm,
    k_pages,
    v_pages,
    seg_hbm,
    o_buf,
    flat,
    q_buf,
    buf,
    seg_ref,
    ext,
    feat,
    top,
    acc,
    local_sem,
    q_sem,
    seg_sem,
    page_send,
    page_recv,
    page_local,
    recv_sem,
    z_sem,
    x_sem,
    c_sem,
):
    rows = q_buf.shape[0]
    planes = n // PLANE
    me = lax.axis_index("seq")
    side = lax.axis_index("mp")
    z = me // PLANE
    k = lax.rem(me, PLANE)
    x = k // 2
    c = lax.rem(k, 2)
    k_core = k + 1 - 2 * c
    k_x = k + 2 - 4 * x
    k_diag = k_core + 2 - 4 * x
    core_dev = z * PLANE + k_core
    x_dev = z * PLANE + k_x
    up_dev = me + PLANE
    has_up = z + 1 < planes

    barrier = pltpu.get_barrier_semaphore()

    def greet(**where):
        pl.semaphore_signal(
            barrier, inc=1, device_id=where, device_id_type=pl.DeviceIdType.MESH
        )

    greet(seq=core_dev)
    greet(seq=x_dev)
    greet(mp=1 - side)

    @pl.when(has_up)
    def _():
        greet(seq=up_dev)

    @pl.when(z > 0)
    def _():
        greet(seq=me - PLANE)

    seg_copy = pltpu.make_async_copy(seg_hbm, seg_ref, seg_sem)
    seg_copy.start()

    def place(h, part):
        return pl.ds(pl.multiple_of(SEG_ROWS + (2 * h + part) * rows, SEG_ROWS), rows)

    @pl.loop(0, heads)
    def _(h):
        cols = pl.ds(pl.multiple_of(h * HD, HD), HD)
        for part, source in enumerate((k_hbm, v_hbm)):
            pltpu.make_async_copy(
                source.at[:, cols], buf.at[k, place(h, part)], local_sem
            ).start()

    pltpu.make_async_copy(q_hbm, q_buf, q_sem).start()
    seg_copy.wait()
    numbers = seg_ref[...].astype(jnp.float32)
    row = lax.broadcasted_iota(jnp.int32, (SEG_ROWS, HD), 0)
    spread = jnp.zeros((SEG_ROWS, HD), jnp.float32)
    for part in range(rows // HD):
        spread = jnp.where(row == part, numbers[part : part + 1, :], spread)
    buf[k, 0:SEG_ROWS] = spread.astype(jnp.bfloat16)
    loaded = buf.at[k, pl.ds(SEG_ROWS, heads * 2 * rows)]
    pltpu.make_async_copy(loaded, loaded, local_sem).wait()

    pl.semaphore_wait(
        barrier, 3 + jnp.where(has_up, 1, 0) + jnp.where(z > 0, 1, 0)
    )

    def send(source, slot, h, part, send_sem, device):
        if part == HEAD:
            where, part = pl.ds(0, SEG_ROWS + rows), 0
        else:
            where = place(h, part)
        return pltpu.make_async_remote_copy(
            src_ref=buf.at[source, where],
            dst_ref=buf.at[slot, where],
            send_sem=send_sem,
            recv_sem=recv_sem.at[slot, h, part],
            device_id={"seq": device},
            device_id_type=pl.DeviceIdType.MESH,
        )

    def up_send(level, h, part):
        source, slot = level * PLANE + k, (level + 1) * PLANE + k
        return send(source, slot, h, part, z_sem.at[level], up_dev)

    def x_send(level, h, part):
        return send(level * PLANE + k, level * PLANE + k, h, part, x_sem.at[level], x_dev)

    def core_send(slot, h, part):
        return send(slot, slot, h, part, c_sem.at[slot], core_dev)

    def all_sent(slot, send_sem):
        pltpu.make_async_remote_copy(
            src_ref=buf.at[slot],
            dst_ref=buf.at[slot],
            send_sem=send_sem,
            recv_sem=recv_sem.at[slot, 0, 0],
            device_id={"seq": core_dev},
            device_id_type=pl.DeviceIdType.MESH,
        ).wait_send()

    def pieces(h, body):
        @pl.when(h == 0)
        def _():
            body(HEAD)

        @pl.when(h > 0)
        def _():
            body(0)

        body(1)

    def arrived(slot, h):
        pieces(h, lambda part: core_send(slot, h, part).wait_recv())

    @pl.loop(0, heads)
    def _(h):
        def begin(part):
            @pl.when(has_up)
            def _():
                up_send(0, h, part).start()

            @pl.when(x == 0)
            def _():
                x_send(0, h, part).start()

            @pl.when(c == 0)
            def _():
                core_send(k, h, part).start()

        pieces(h, begin)

    slots = flat.shape[1]
    width = heads * HD

    def page_copies():
        out = []
        for kv, pages in enumerate((k_pages, v_pages)):
            dst = flat.at[
                :, :, pl.ds(pl.multiple_of(kv * 2 * width + side * width, HD), width)
            ]
            away = pages.at[:, pl.ds(pl.multiple_of((1 - side) * slots, slots), slots), :]
            here = pages.at[:, pl.ds(pl.multiple_of(side * slots, slots), slots), :]
            out.append(
                pltpu.make_async_remote_copy(
                    src_ref=away,
                    dst_ref=dst,
                    send_sem=page_send.at[kv],
                    recv_sem=page_recv.at[kv],
                    device_id={"mp": 1 - side},
                    device_id_type=pl.DeviceIdType.MESH,
                )
            )
            out.append(pltpu.make_async_copy(here, dst, page_local.at[kv]))
        return out

    for copy in page_copies():
        copy.start()

    def clear(first, count=PLANE):
        @pl.loop(first, first + count)
        def _(slot):
            buf[slot, 0:SEG_ROWS] = jnp.zeros((SEG_ROWS, HD), buf.dtype)

            @pl.loop(0, 2 * heads)
            def _(half):
                buf[slot, place(0, half)] = jnp.zeros((rows, HD), buf.dtype)

    @pl.when(c == 0)
    def _():
        clear(k_core, 1)

    @pl.when(z < 1)
    def _():
        clear(PLANE)

    @pl.when(z < 2)
    def _():
        clear(2 * PLANE)

    def build_ext(slot, present):
        seg = buf[slot, 0:SEG_ROWS].astype(jnp.float32)
        other = jnp.where(present, 0.0, 1.0)
        number = lax.broadcasted_iota(jnp.int32, (HD, HD), 0).astype(jnp.float32)
        for part in range(rows // HD):
            hot = jnp.where(number == seg[part : part + 1, :], 1.0, other)
            ext[slot, part * HD : (part + 1) * HD, :] = hot.T.astype(jnp.bfloat16)

    build_ext(k, True)
    feat[...] = ((ext[k].astype(jnp.float32) - 1.0) * BIG).astype(jnp.bfloat16)
    ones = jnp.ones((rows, HD), jnp.bfloat16)

    def attend(slot_list, h, first, last):
        keys = jnp.concatenate(
            [jnp.concatenate([buf[s, place(h, 0)], ext[s]], axis=1) for s in slot_list],
            axis=0,
        )
        vals = jnp.concatenate(
            [jnp.concatenate([buf[s, place(h, 1)], ones], axis=1) for s in slot_list],
            axis=0,
        )

        def columns(g):
            return pl.ds(pl.multiple_of((h * group + g) * HD, HD), HD)

        def scores(g):
            query = jnp.concatenate([q_buf[:, columns(g)], feat[...]], axis=1)
            return lax.dot_general(query, keys, NT, preferred_element_type=jnp.float32)

        following = scores(0)
        for g in range(group):
            score = following
            if g + 1 < group:
                following = scores(g + 1)
            if first:
                later = lax.broadcasted_iota(jnp.int32, score.shape, 1) > (
                    lax.broadcasted_iota(jnp.int32, score.shape, 0) + c * rows
                )
                score = jnp.where(later, -BIG, score)
            best = jnp.max(score, axis=1, keepdims=True)
            if not first:
                old = top[h, g]
                best = jnp.maximum(old, best)
            weight = jnp.exp2((score - best) * EXP_SCALE).astype(jnp.bfloat16)
            new = lax.dot_general(weight, vals, NN, preferred_element_type=jnp.float32)
            if not first:
                new = new + acc[h, g] * jnp.exp2((old - best) * EXP_SCALE)
            if last:
                o_buf[:, columns(g)] = (new[:, :HD] / new[:, HD:]).astype(jnp.bfloat16)
            else:
                acc[h, g] = new
                top[h, g] = best

    def relay(step):
        phase = step // heads
        h = lax.rem(step, heads)
        z_level = 1 + phase
        x_level = z_level - x

        @pl.when(z >= z_level)
        def _():
            slot = z_level * PLANE + k

            def pass_on(part):
                core_send(slot, h, part).wait_recv()

                @pl.when((x == 1) | (phase == 0))
                def _():
                    x_send(z_level, h, part).start()

                core_send(slot, h, part).start()

                @pl.when((phase == 0) & has_up)
                def _():
                    up_send(1, h, part).start()

            pieces(h, pass_on)

        @pl.when(z >= x_level)
        def _():
            slot = x_level * PLANE + k_x

            def pass_on(part):
                core_send(slot, h, part).wait_recv()
                core_send(slot, h, part).start()

            pieces(h, pass_on)

    pltpu.make_async_copy(q_hbm, q_buf, q_sem).wait()
    steps = 2 * heads
    chip = [k - c, k - c + 1]

    @pl.loop(0, heads)
    def _(h):
        @pl.when(h == heads - 1)
        def _():
            relay(0)

        @pl.when(c == 1)
        def _():
            arrived(k_core, h)

        @pl.when(h == 0)
        def _():
            build_ext(k_core, True)

        attend(chip, h, True, False)

    @pl.loop(0, steps)
    def _(step):
        phase = step // heads
        h = lax.rem(step, heads)
        z_level = 1 + phase
        x_level = z_level - x

        @pl.when(step + 1 < steps)
        def _():
            relay(step + 1)

        @pl.when(z >= z_level)
        def _():
            arrived(z_level * PLANE + k_core, h)

        @pl.when(z >= x_level)
        def _():
            arrived(x_level * PLANE + k_diag, h)

        slot_list = [
            (x_level if place < 2 else z_level) * PLANE + place for place in range(PLANE)
        ]

        @pl.when(h == 0)
        def _():
            for place, slot in enumerate(slot_list):
                build_ext(slot, z >= (x_level if place < 2 else z_level))

        @pl.when(phase == 0)
        def _():
            attend(slot_list, h, False, False)

        @pl.when(phase == 1)
        def _():
            attend(slot_list, h, False, True)

    for copy in page_copies():
        copy.wait()

    @pl.when(has_up)
    def _():
        all_sent(k, z_sem.at[0])

    @pl.when(has_up & (z >= 1))
    def _():
        all_sent(PLANE + k, z_sem.at[1])

    @pl.when(x == 0)
    def _():
        all_sent(k, x_sem.at[0])

    @pl.when(z >= 1)
    def _():
        all_sent(PLANE + k, x_sem.at[1])

    @pl.when((z >= 2) & (x == 1))
    def _():
        all_sent(2 * PLANE + k, x_sem.at[2])

    @pl.when(c == 0)
    def _():
        all_sent(k, c_sem.at[k])

    for phase in range(2):
        level = 1 + phase

        @pl.when(z >= level)
        def _():
            all_sent(level * PLANE + k, c_sem.at[level * PLANE + k])

        @pl.when(z >= level - x)
        def _():
            slot = (level - x) * PLANE + k_x
            all_sent(slot, c_sem.at[slot])


def place_kernel(slots_ref, flat, context, context_hbm, cache_hbm, sems, context_sem):
    count = flat.shape[0]
    base = lax.axis_index("seq") * count
    whole = pltpu.make_async_copy(context, context_hbm, context_sem)
    whole.start()

    def copy(p):
        return pltpu.make_async_copy(
            flat.at[p], cache_hbm.at[slots_ref[p] - base], sems
        )

    for p in range(count):
        copy(p).start()
    pltpu.make_async_copy(flat, cache_hbm, sems).wait()
    whole.wait()


def in_hbm(array):
    return pltpu.with_memory_space_constraint(array, pltpu.HBM)


def local(n, queries, keys, values, segment_ids, page_slots):
    rows = queries.shape[0]
    heads = keys.shape[1] // HD
    group = queries.shape[1] // HD // heads
    page_dev = page_slots.shape[0]
    page = rows // page_dev
    any_spec = pl.BlockSpec(memory_space=pl.ANY)
    hbm_spec = pl.BlockSpec(memory_space=pltpu.HBM)
    vmem_spec = pl.BlockSpec(memory_space=pltpu.VMEM)
    slots = LEVELS * PLANE
    context_type = jax.ShapeDtypeStruct(queries.shape, jnp.bfloat16)
    cache_type = jax.ShapeDtypeStruct((page_dev, page // 2, 4 * heads * HD), jnp.bfloat16)
    context, flat = pl.pallas_call(
        functools.partial(kernel, n, heads, group),
        out_shape=(context_type, cache_type),
        in_specs=[hbm_spec] * 6,
        out_specs=(vmem_spec, vmem_spec),
        scratch_shapes=[
            pltpu.VMEM(queries.shape, jnp.bfloat16),
            pltpu.VMEM((slots, SEG_ROWS + heads * 2 * rows, HD), jnp.bfloat16),
            pltpu.VMEM((rows // HD, HD), jnp.int32),
            pltpu.VMEM((slots, rows, HD), jnp.bfloat16),
            pltpu.VMEM((rows, HD), jnp.bfloat16),
            pltpu.VMEM((heads, group, rows, 1), jnp.float32),
            pltpu.VMEM((heads, group, rows, 2 * HD), jnp.float32),
            pltpu.SemaphoreType.DMA,
            pltpu.SemaphoreType.DMA,
            pltpu.SemaphoreType.DMA,
            pltpu.SemaphoreType.DMA((2,)),
            pltpu.SemaphoreType.DMA((2,)),
            pltpu.SemaphoreType.DMA((2,)),
            pltpu.SemaphoreType.DMA((slots, heads, 2)),
            pltpu.SemaphoreType.DMA((LEVELS,)),
            pltpu.SemaphoreType.DMA((LEVELS,)),
            pltpu.SemaphoreType.DMA((slots,)),
        ],
        compiler_params=pltpu.CompilerParams(
            collective_id=0, has_side_effects=True, vmem_limit_bytes=36 * 2**20
        ),
    )(
        in_hbm(queries),
        in_hbm(keys),
        in_hbm(values),
        in_hbm(keys.reshape(page_dev, page, heads * HD)),
        in_hbm(values.reshape(page_dev, page, heads * HD)),
        in_hbm(segment_ids.reshape(rows // HD, HD)),
    )
    return pl.pallas_call(
        place_kernel,
        out_shape=(context_type, cache_type),
        in_specs=[pl.BlockSpec(memory_space=pltpu.SMEM), vmem_spec, vmem_spec],
        out_specs=(any_spec, any_spec),
        scratch_shapes=[pltpu.SemaphoreType.DMA, pltpu.SemaphoreType.DMA],
        compiler_params=pltpu.CompilerParams(vmem_limit_bytes=8 * 2**20),
    )(page_slots, flat, context)


def solution(mesh):
    placed = (P("seq", "mp"), P("seq", "mp"), P("seq", "mp"), P("seq"), P("seq"))
    return jax.shard_map(
        functools.partial(local, mesh.shape["seq"]),
        mesh=mesh,
        in_specs=placed,
        out_specs=(P("seq", "mp"), P("seq", "mp", None)),
        check_vma=False,
    )
```

```python
import functools
import math

import jax
import jax.numpy as jnp
from jax import lax
from jax.experimental import pallas as pl
from jax.experimental.pallas import tpu as pltpu
from jax.sharding import PartitionSpec as P

HD = 128
LMAX = 2048
PLANE = 4
LEVELS = 3
BIG = 2.0**30
HEAD = 2
SEG_ROWS = 16
EXP_SCALE = math.log2(math.e) / math.sqrt(HD)
NT = (((1,), (1,)), ((), ()))
NN = (((1,), (0,)), ((), ()))


def kernel(
    n,
    heads,
    group,
    q_hbm,
    k_hbm,
    v_hbm,
    k_pages,
    v_pages,
    seg_hbm,
    o_buf,
    flat,
    q_buf,
    buf,
    seg_ref,
    ext,
    feat,
    top,
    fade,
    weights,
    acc,
    local_sem,
    q_sem,
    seg_sem,
    page_send,
    page_recv,
    page_local,
    recv_sem,
    z_sem,
    x_sem,
    c_sem,
):
    rows = q_buf.shape[0]
    planes = n // PLANE
    me = lax.axis_index("seq")
    side = lax.axis_index("mp")
    z = me // PLANE
    k = lax.rem(me, PLANE)
    x = k // 2
    c = lax.rem(k, 2)
    k_core = k + 1 - 2 * c
    k_x = k_core + 2 - 4 * x
    k_diag = k + 2 - 4 * x
    core_dev = z * PLANE + k_core
    x_dev = z * PLANE + k_x
    up_dev = me + PLANE
    has_up = z + 1 < planes

    barrier = pltpu.get_barrier_semaphore()

    def greet(**where):
        pl.semaphore_signal(
            barrier, inc=1, device_id=where, device_id_type=pl.DeviceIdType.MESH
        )

    greet(seq=core_dev)
    greet(seq=x_dev)
    greet(mp=1 - side)

    @pl.when(has_up)
    def _():
        greet(seq=up_dev)

    @pl.when(z > 0)
    def _():
        greet(seq=me - PLANE)

    seg_copy = pltpu.make_async_copy(seg_hbm, seg_ref, seg_sem)
    seg_copy.start()

    def place(h, part):
        return pl.ds(pl.multiple_of(SEG_ROWS + (2 * h + part) * rows, SEG_ROWS), rows)

    @pl.loop(0, heads)
    def _(h):
        cols = pl.ds(pl.multiple_of(h * HD, HD), HD)
        for part, source in enumerate((k_hbm, v_hbm)):
            pltpu.make_async_copy(
                source.at[:, cols], buf.at[k, place(h, part)], local_sem
            ).start()

    pltpu.make_async_copy(q_hbm, q_buf, q_sem).start()
    seg_copy.wait()
    numbers = seg_ref[...].astype(jnp.float32)
    row = lax.broadcasted_iota(jnp.int32, (SEG_ROWS, HD), 0)
    spread = jnp.zeros((SEG_ROWS, HD), jnp.float32)
    for part in range(rows // HD):
        spread = jnp.where(row == part, numbers[part : part + 1, :], spread)
    buf[k, 0:SEG_ROWS] = spread.astype(jnp.bfloat16)
    loaded = buf.at[k, pl.ds(SEG_ROWS, heads * 2 * rows)]
    pltpu.make_async_copy(loaded, loaded, local_sem).wait()

    pl.semaphore_wait(
        barrier, 3 + jnp.where(has_up, 1, 0) + jnp.where(z > 0, 1, 0)
    )

    def send(source, slot, h, part, send_sem, device):
        if part == HEAD:
            where, part = pl.ds(0, SEG_ROWS + rows), 0
        else:
            where = place(h, part)
        return pltpu.make_async_remote_copy(
            src_ref=buf.at[source, where],
            dst_ref=buf.at[slot, where],
            send_sem=send_sem,
            recv_sem=recv_sem.at[slot, h, part],
            device_id={"seq": device},
            device_id_type=pl.DeviceIdType.MESH,
        )

    def up_send(level, h, part):
        source, slot = level * PLANE + k, (level + 1) * PLANE + k
        return send(source, slot, h, part, z_sem.at[level], up_dev)

    def x_send(level, h, part):
        return send(level * PLANE + k, level * PLANE + k, h, part, x_sem.at[level], x_dev)

    def core_send(slot, h, part):
        return send(slot, slot, h, part, c_sem.at[slot], core_dev)

    def all_sent(slot, send_sem):
        pltpu.make_async_remote_copy(
            src_ref=buf.at[slot],
            dst_ref=buf.at[slot],
            send_sem=send_sem,
            recv_sem=recv_sem.at[slot, 0, 0],
            device_id={"seq": core_dev},
            device_id_type=pl.DeviceIdType.MESH,
        ).wait_send()

    def piece(h, part, body):
        if part == 0:
            @pl.when(h == 0)
            def _():
                body(HEAD)

            @pl.when(h > 0)
            def _():
                body(0)
        else:
            body(1)

    def arrived(slot, h, part):
        piece(h, part, lambda p: core_send(slot, h, p).wait_recv())

    @pl.loop(0, heads)
    def _(h):
        def begin(part):
            @pl.when(has_up)
            def _():
                up_send(0, h, part).start()

            @pl.when(x == 0)
            def _():
                x_send(0, h, part).start()

            @pl.when(c == 0)
            def _():
                core_send(k, h, part).start()

        piece(h, 0, begin)
        piece(h, 1, begin)

    slots = flat.shape[1]
    width = heads * HD

    def page_copies():
        out = []
        for kv, pages in enumerate((k_pages, v_pages)):
            dst = flat.at[
                :, :, pl.ds(pl.multiple_of(kv * 2 * width + side * width, HD), width)
            ]
            away = pages.at[:, pl.ds(pl.multiple_of((1 - side) * slots, slots), slots), :]
            here = pages.at[:, pl.ds(pl.multiple_of(side * slots, slots), slots), :]
            out.append(
                pltpu.make_async_remote_copy(
                    src_ref=away,
                    dst_ref=dst,
                    send_sem=page_send.at[kv],
                    recv_sem=page_recv.at[kv],
                    device_id={"mp": 1 - side},
                    device_id_type=pl.DeviceIdType.MESH,
                )
            )
            out.append(pltpu.make_async_copy(here, dst, page_local.at[kv]))
        return out

    for copy in page_copies():
        copy.start()

    def clear(first, count=PLANE):
        @pl.loop(first, first + count)
        def _(slot):
            buf[slot, 0:SEG_ROWS] = jnp.zeros((SEG_ROWS, HD), buf.dtype)

            @pl.loop(0, 2 * heads)
            def _(half):
                buf[slot, place(0, half)] = jnp.zeros((rows, HD), buf.dtype)

    @pl.when(c == 0)
    def _():
        clear(k_core, 1)

    @pl.when(z < 1)
    def _():
        clear(PLANE)

    @pl.when(z < 2)
    def _():
        clear(2 * PLANE)

    def build_ext(slot, present):
        seg = buf[slot, 0:SEG_ROWS].astype(jnp.float32)
        other = jnp.where(present, 0.0, 1.0)
        number = lax.broadcasted_iota(jnp.int32, (HD, HD), 0).astype(jnp.float32)
        for part in range(rows // HD):
            hot = jnp.where(number == seg[part : part + 1, :], 1.0, other)
            ext[slot, part * HD : (part + 1) * HD, :] = hot.T.astype(jnp.bfloat16)

    build_ext(k, True)
    feat[...] = ((ext[k].astype(jnp.float32) - 1.0) * BIG).astype(jnp.bfloat16)
    ones = jnp.ones((rows, HD), jnp.bfloat16)

    def columns(h, g):
        return pl.ds(pl.multiple_of((h * group + g) * HD, HD), HD)

    def weigh(slot_list, h, first):
        width = len(slot_list) * rows
        keys = jnp.concatenate(
            [jnp.concatenate([buf[s, place(h, 0)], ext[s]], axis=1) for s in slot_list],
            axis=0,
        )

        def scores(g):
            query = jnp.concatenate([q_buf[:, columns(h, g)], feat[...]], axis=1)
            return lax.dot_general(query, keys, NT, preferred_element_type=jnp.float32)

        following = scores(0)
        for g in range(group):
            score = following
            if g + 1 < group:
                following = scores(g + 1)
            if first:
                later = lax.broadcasted_iota(jnp.int32, score.shape, 1) > (
                    lax.broadcasted_iota(jnp.int32, score.shape, 0) + c * rows
                )
                score = jnp.where(later, -BIG, score)
            best = jnp.max(score, axis=1, keepdims=True)
            if not first:
                old = top[h, g]
                best = jnp.maximum(old, best)
                fade[g] = jnp.exp2((old - best) * EXP_SCALE)
            top[h, g] = best
            weight = jnp.exp2((score - best) * EXP_SCALE).astype(jnp.bfloat16)
            weights[g, :, 0:width] = weight

    def add_up(slot_list, h, first, last):
        width = len(slot_list) * rows
        vals = jnp.concatenate(
            [jnp.concatenate([buf[s, place(h, 1)], ones], axis=1) for s in slot_list],
            axis=0,
        )
        for g in range(group):
            new = lax.dot_general(
                weights[g, :, 0:width], vals, NN, preferred_element_type=jnp.float32
            )
            if not first:
                new = new + acc[h, g] * fade[g]
            if last:
                o_buf[:, columns(h, g)] = (new[:, :HD] / new[:, HD:]).astype(jnp.bfloat16)
            else:
                acc[h, g] = new

    def relay(step, part):
        phase = step // heads
        h = lax.rem(step, heads)
        z_level = 1 + phase
        x_level = z_level - x

        @pl.when(z >= z_level)
        def _():
            slot = z_level * PLANE + k

            def pass_on(p):
                core_send(slot, h, p).wait_recv()

                @pl.when((x == 1) | (phase == 0))
                def _():
                    x_send(z_level, h, p).start()

                core_send(slot, h, p).start()

                @pl.when((phase == 0) & has_up)
                def _():
                    up_send(1, h, p).start()

            piece(h, part, pass_on)

        @pl.when(z >= x_level)
        def _():
            slot = x_level * PLANE + k_x

            def pass_on(p):
                core_send(slot, h, p).wait_recv()
                core_send(slot, h, p).start()

            piece(h, part, pass_on)

    def from_core(step, part):
        phase = step // heads
        h = lax.rem(step, heads)
        z_level = 1 + phase
        x_level = z_level - x

        @pl.when(z >= z_level)
        def _():
            arrived(z_level * PLANE + k_core, h, part)

        @pl.when(z >= x_level)
        def _():
            arrived(x_level * PLANE + k_diag, h, part)

    pltpu.make_async_copy(q_hbm, q_buf, q_sem).wait()
    steps = 2 * heads
    chip = [k - c, k - c + 1]

    @pl.loop(0, heads)
    def _(h):
        @pl.when(h == heads - 1)
        def _():
            relay(0, 0)

        @pl.when(c == 1)
        def _():
            arrived(k_core, h, 0)
            arrived(k_core, h, 1)

        @pl.when(h == 0)
        def _():
            build_ext(k_core, True)

        weigh(chip, h, True)
        add_up(chip, h, True, False)

    @pl.loop(0, steps)
    def _(step):
        phase = step // heads
        h = lax.rem(step, heads)
        z_level = 1 + phase
        x_level = z_level - x
        slot_list = [
            (x_level if spot < 2 else z_level) * PLANE + spot for spot in range(PLANE)
        ]

        relay(step, 1)
        from_core(step, 0)

        @pl.when(h == 0)
        def _():
            for spot, slot in enumerate(slot_list):
                build_ext(slot, z >= (x_level if spot < 2 else z_level))

        weigh(slot_list, h, False)

        @pl.when(step + 1 < steps)
        def _():
            relay(step + 1, 0)

        from_core(step, 1)

        @pl.when(phase == 0)
        def _():
            add_up(slot_list, h, False, False)

        @pl.when(phase == 1)
        def _():
            add_up(slot_list, h, False, True)

    for copy in page_copies():
        copy.wait()

    @pl.when(has_up)
    def _():
        all_sent(k, z_sem.at[0])

    @pl.when(has_up & (z >= 1))
    def _():
        all_sent(PLANE + k, z_sem.at[1])

    @pl.when(x == 0)
    def _():
        all_sent(k, x_sem.at[0])

    @pl.when(z >= 1)
    def _():
        all_sent(PLANE + k, x_sem.at[1])

    @pl.when((z >= 2) & (x == 1))
    def _():
        all_sent(2 * PLANE + k, x_sem.at[2])

    @pl.when(c == 0)
    def _():
        all_sent(k, c_sem.at[k])

    for phase in range(2):
        level = 1 + phase

        @pl.when(z >= level)
        def _():
            all_sent(level * PLANE + k, c_sem.at[level * PLANE + k])

        @pl.when(z >= level - x)
        def _():
            slot = (level - x) * PLANE + k_x
            all_sent(slot, c_sem.at[slot])


def place_kernel(slots_ref, flat, context, context_hbm, cache_hbm, sems, context_sem):
    count = flat.shape[0]
    base = lax.axis_index("seq") * count
    whole = pltpu.make_async_copy(context, context_hbm, context_sem)
    whole.start()

    def copy(p):
        return pltpu.make_async_copy(
            flat.at[p], cache_hbm.at[slots_ref[p] - base], sems
        )

    for p in range(count):
        copy(p).start()
    pltpu.make_async_copy(flat, cache_hbm, sems).wait()
    whole.wait()


def in_hbm(array):
    return pltpu.with_memory_space_constraint(array, pltpu.HBM)


def local(n, queries, keys, values, segment_ids, page_slots):
    rows = queries.shape[0]
    heads = keys.shape[1] // HD
    group = queries.shape[1] // HD // heads
    page_dev = page_slots.shape[0]
    page = rows // page_dev
    any_spec = pl.BlockSpec(memory_space=pl.ANY)
    hbm_spec = pl.BlockSpec(memory_space=pltpu.HBM)
    vmem_spec = pl.BlockSpec(memory_space=pltpu.VMEM)
    slots = LEVELS * PLANE
    context_type = jax.ShapeDtypeStruct(queries.shape, jnp.bfloat16)
    cache_type = jax.ShapeDtypeStruct((page_dev, page // 2, 4 * heads * HD), jnp.bfloat16)
    context, flat = pl.pallas_call(
        functools.partial(kernel, n, heads, group),
        out_shape=(context_type, cache_type),
        in_specs=[hbm_spec] * 6,
        out_specs=(vmem_spec, vmem_spec),
        scratch_shapes=[
            pltpu.VMEM(queries.shape, jnp.bfloat16),
            pltpu.VMEM((slots, SEG_ROWS + heads * 2 * rows, HD), jnp.bfloat16),
            pltpu.VMEM((rows // HD, HD), jnp.int32),
            pltpu.VMEM((slots, rows, HD), jnp.bfloat16),
            pltpu.VMEM((rows, HD), jnp.bfloat16),
            pltpu.VMEM((heads, group, rows, 1), jnp.float32),
            pltpu.VMEM((group, rows, 1), jnp.float32),
            pltpu.VMEM((group, rows, PLANE * rows), jnp.bfloat16),
            pltpu.VMEM((heads, group, rows, 2 * HD), jnp.float32),
            pltpu.SemaphoreType.DMA,
            pltpu.SemaphoreType.DMA,
            pltpu.SemaphoreType.DMA,
            pltpu.SemaphoreType.DMA((2,)),
            pltpu.SemaphoreType.DMA((2,)),
            pltpu.SemaphoreType.DMA((2,)),
            pltpu.SemaphoreType.DMA((slots, heads, 2)),
            pltpu.SemaphoreType.DMA((LEVELS,)),
            pltpu.SemaphoreType.DMA((LEVELS,)),
            pltpu.SemaphoreType.DMA((slots,)),
        ],
        compiler_params=pltpu.CompilerParams(
            collective_id=0, has_side_effects=True, vmem_limit_bytes=36 * 2**20
        ),
    )(
        in_hbm(queries),
        in_hbm(keys),
        in_hbm(values),
        in_hbm(keys.reshape(page_dev, page, heads * HD)),
        in_hbm(values.reshape(page_dev, page, heads * HD)),
        in_hbm(segment_ids.reshape(rows // HD, HD)),
    )
    return pl.pallas_call(
        place_kernel,
        out_shape=(context_type, cache_type),
        in_specs=[pl.BlockSpec(memory_space=pltpu.SMEM), vmem_spec, vmem_spec],
        out_specs=(any_spec, any_spec),
        scratch_shapes=[pltpu.SemaphoreType.DMA, pltpu.SemaphoreType.DMA],
        compiler_params=pltpu.CompilerParams(vmem_limit_bytes=8 * 2**20),
    )(page_slots, flat, context)


def solution(mesh):
    placed = (P("seq", "mp"), P("seq", "mp"), P("seq", "mp"), P("seq"), P("seq"))
    return jax.shard_map(
        functools.partial(local, mesh.shape["seq"]),
        mesh=mesh,
        in_specs=placed,
        out_specs=(P("seq", "mp"), P("seq", "mp", None)),
        check_vma=False,
    )
```

```python
import functools
import math

import jax
import jax.numpy as jnp
from jax import lax
from jax.experimental import pallas as pl
from jax.experimental.pallas import tpu as pltpu
from jax.sharding import PartitionSpec as P

HD = 128
LMAX = 2048
PLANE = 4
LEVELS = 3
BIG = 2.0**30
HEAD = 2
SEG_ROWS = 16
EXP_SCALE = math.log2(math.e) / math.sqrt(HD)
NT = (((1,), (1,)), ((), ()))
NN = (((1,), (0,)), ((), ()))


def kernel(
    n,
    heads,
    group,
    q_hbm,
    k_hbm,
    v_hbm,
    k_pages,
    v_pages,
    seg_hbm,
    o_buf,
    flat,
    q_buf,
    buf,
    seg_ref,
    ext,
    feat,
    top,
    fade,
    weights,
    acc,
    local_sem,
    q_sem,
    seg_sem,
    page_send,
    page_recv,
    page_local,
    recv_sem,
    z_sem,
    x_sem,
    c_sem,
):
    rows = q_buf.shape[0]
    planes = n // PLANE
    me = lax.axis_index("seq")
    side = lax.axis_index("mp")
    z = me // PLANE
    k = lax.rem(me, PLANE)
    x = k // 2
    c = lax.rem(k, 2)
    k_core = k + 1 - 2 * c
    k_x = k_core + 2 - 4 * x
    k_diag = k + 2 - 4 * x
    core_dev = z * PLANE + k_core
    x_dev = z * PLANE + k_x
    up_dev = me + PLANE
    has_up = z + 1 < planes

    barrier = pltpu.get_barrier_semaphore()

    def greet(**where):
        pl.semaphore_signal(
            barrier, inc=1, device_id=where, device_id_type=pl.DeviceIdType.MESH
        )

    greet(seq=core_dev)
    greet(seq=x_dev)
    greet(mp=1 - side)

    @pl.when(has_up)
    def _():
        greet(seq=up_dev)

    @pl.when(z > 0)
    def _():
        greet(seq=me - PLANE)

    seg_copy = pltpu.make_async_copy(seg_hbm, seg_ref, seg_sem)
    seg_copy.start()

    def place(h, part):
        return pl.ds(pl.multiple_of(SEG_ROWS + (2 * h + part) * rows, SEG_ROWS), rows)

    @pl.loop(0, heads)
    def _(h):
        cols = pl.ds(pl.multiple_of(h * HD, HD), HD)
        for part, source in enumerate((k_hbm, v_hbm)):
            pltpu.make_async_copy(
                source.at[:, cols], buf.at[k, place(h, part)], local_sem
            ).start()

    pltpu.make_async_copy(q_hbm, q_buf, q_sem).start()
    seg_copy.wait()
    numbers = seg_ref[...].astype(jnp.float32)
    row = lax.broadcasted_iota(jnp.int32, (SEG_ROWS, HD), 0)
    spread = jnp.zeros((SEG_ROWS, HD), jnp.float32)
    for part in range(rows // HD):
        spread = jnp.where(row == part, numbers[part : part + 1, :], spread)
    buf[k, 0:SEG_ROWS] = spread.astype(jnp.bfloat16)
    loaded = buf.at[k, pl.ds(SEG_ROWS, heads * 2 * rows)]
    pltpu.make_async_copy(loaded, loaded, local_sem).wait()

    pl.semaphore_wait(
        barrier, 3 + jnp.where(has_up, 1, 0) + jnp.where(z > 0, 1, 0)
    )

    def send(source, slot, h, part, send_sem, device):
        if part == HEAD:
            where, part = pl.ds(0, SEG_ROWS + rows), 0
        else:
            where = place(h, part)
        return pltpu.make_async_remote_copy(
            src_ref=buf.at[source, where],
            dst_ref=buf.at[slot, where],
            send_sem=send_sem,
            recv_sem=recv_sem.at[slot, h, part],
            device_id={"seq": device},
            device_id_type=pl.DeviceIdType.MESH,
        )

    def up_send(level, h, part):
        source, slot = level * PLANE + k, (level + 1) * PLANE + k
        return send(source, slot, h, part, z_sem.at[level], up_dev)

    def side_send():
        source, slot = PLANE + k_x, 2 * PLANE + k_x
        return send(source, slot, heads - 1, 1, z_sem.at[2], up_dev)

    def x_send(level, h, part):
        return send(level * PLANE + k, level * PLANE + k, h, part, x_sem.at[level], x_dev)

    def core_send(slot, h, part):
        return send(slot, slot, h, part, c_sem.at[slot], core_dev)

    def all_sent(slot, send_sem, less=0):
        sent = buf.at[slot, pl.ds(0, buf.shape[1] - less)]
        pltpu.make_async_remote_copy(
            src_ref=sent,
            dst_ref=sent,
            send_sem=send_sem,
            recv_sem=recv_sem.at[slot, 0, 0],
            device_id={"seq": core_dev},
            device_id_type=pl.DeviceIdType.MESH,
        ).wait_send()

    def piece(h, part, body):
        if part == 0:
            @pl.when(h == 0)
            def _():
                body(HEAD)

            @pl.when(h > 0)
            def _():
                body(0)
        else:
            body(1)

    def arrived(slot, h, part):
        piece(h, part, lambda p: core_send(slot, h, p).wait_recv())

    @pl.loop(0, heads)
    def _(h):
        def begin(part):
            @pl.when(has_up)
            def _():
                up_send(0, h, part).start()

            @pl.when(x == 0)
            def _():
                x_send(0, h, part).start()

            @pl.when(c == 0)
            def _():
                core_send(k, h, part).start()

        piece(h, 0, begin)
        piece(h, 1, begin)

    slots = flat.shape[1]
    width = heads * HD

    def page_copies():
        out = []
        for kv, pages in enumerate((k_pages, v_pages)):
            dst = flat.at[
                :, :, pl.ds(pl.multiple_of(kv * 2 * width + side * width, HD), width)
            ]
            away = pages.at[:, pl.ds(pl.multiple_of((1 - side) * slots, slots), slots), :]
            here = pages.at[:, pl.ds(pl.multiple_of(side * slots, slots), slots), :]
            out.append(
                pltpu.make_async_remote_copy(
                    src_ref=away,
                    dst_ref=dst,
                    send_sem=page_send.at[kv],
                    recv_sem=page_recv.at[kv],
                    device_id={"mp": 1 - side},
                    device_id_type=pl.DeviceIdType.MESH,
                )
            )
            out.append(pltpu.make_async_copy(here, dst, page_local.at[kv]))
        return out

    for copy in page_copies():
        copy.start()

    def clear(first, count=PLANE):
        @pl.loop(first, first + count)
        def _(slot):
            buf[slot, 0:SEG_ROWS] = jnp.zeros((SEG_ROWS, HD), buf.dtype)

            @pl.loop(0, 2 * heads)
            def _(half):
                buf[slot, place(0, half)] = jnp.zeros((rows, HD), buf.dtype)

    @pl.when(c == 0)
    def _():
        clear(k_core, 1)

    @pl.when(z < 1)
    def _():
        clear(PLANE)

    @pl.when(z < 2)
    def _():
        clear(2 * PLANE)

    def build_ext(slot, present):
        seg = buf[slot, 0:SEG_ROWS].astype(jnp.float32)
        other = jnp.where(present, 0.0, 1.0)
        number = lax.broadcasted_iota(jnp.int32, (HD, HD), 0).astype(jnp.float32)
        for part in range(rows // HD):
            hot = jnp.where(number == seg[part : part + 1, :], 1.0, other)
            ext[slot, part * HD : (part + 1) * HD, :] = hot.T.astype(jnp.bfloat16)

    build_ext(k, True)
    feat[...] = ((ext[k].astype(jnp.float32) - 1.0) * BIG).astype(jnp.bfloat16)
    ones = jnp.ones((rows, HD), jnp.bfloat16)

    def columns(h, g):
        return pl.ds(pl.multiple_of((h * group + g) * HD, HD), HD)

    def weigh(slot_list, h, first):
        width = len(slot_list) * rows
        keys = jnp.concatenate(
            [jnp.concatenate([buf[s, place(h, 0)], ext[s]], axis=1) for s in slot_list],
            axis=0,
        )

        def scores(g):
            query = jnp.concatenate([q_buf[:, columns(h, g)], feat[...]], axis=1)
            return lax.dot_general(query, keys, NT, preferred_element_type=jnp.float32)

        following = scores(0)
        for g in range(group):
            score = following
            if g + 1 < group:
                following = scores(g + 1)
            if first:
                later = lax.broadcasted_iota(jnp.int32, score.shape, 1) > (
                    lax.broadcasted_iota(jnp.int32, score.shape, 0) + c * rows
                )
                score = jnp.where(later, -BIG, score)
            best = jnp.max(score, axis=1, keepdims=True)
            if not first:
                old = top[h, g]
                best = jnp.maximum(old, best)
                fade[g] = jnp.exp2((old - best) * EXP_SCALE)
            top[h, g] = best
            weight = jnp.exp2((score - best) * EXP_SCALE).astype(jnp.bfloat16)
            weights[g, :, 0:width] = weight

    def add_up(slot_list, h, first, last):
        width = len(slot_list) * rows
        vals = jnp.concatenate(
            [jnp.concatenate([buf[s, place(h, 1)], ones], axis=1) for s in slot_list],
            axis=0,
        )
        for g in range(group):
            new = lax.dot_general(
                weights[g, :, 0:width], vals, NN, preferred_element_type=jnp.float32
            )
            if not first:
                new = new + acc[h, g] * fade[g]
            if last:
                o_buf[:, columns(h, g)] = (new[:, :HD] / new[:, HD:]).astype(jnp.bfloat16)
            else:
                acc[h, g] = new

    def relay(step, part):
        phase = step // heads
        h = lax.rem(step, heads)
        z_level = 1 + phase
        x_level = z_level - x

        @pl.when(z >= z_level)
        def _():
            slot = z_level * PLANE + k

            def pass_on(p):
                core_send(slot, h, p).wait_recv()

                last_v = p == 1 and (phase == 1) & (h == heads - 1)

                @pl.when(((x == 1) | (phase == 0)) & jnp.logical_not(last_v))
                def _():
                    x_send(z_level, h, p).start()

                core_send(slot, h, p).start()

                @pl.when((phase == 0) & has_up)
                def _():
                    up_send(1, h, p).start()

            piece(h, part, pass_on)

        @pl.when(z >= x_level)
        def _():
            slot = x_level * PLANE + k_x

            def pass_on(p):
                core_send(slot, h, p).wait_recv()
                core_send(slot, h, p).start()

                if p == 1:
                    @pl.when((x == 0) & (phase == 0) & (h == heads - 1) & has_up)
                    def _():
                        side_send().start()

            piece(h, part, pass_on)

    def from_core(step, part):
        phase = step // heads
        h = lax.rem(step, heads)
        z_level = 1 + phase
        x_level = z_level - x

        @pl.when(z >= z_level)
        def _():
            arrived(z_level * PLANE + k_core, h, part)

        @pl.when(z >= x_level)
        def _():
            arrived(x_level * PLANE + k_diag, h, part)

    pltpu.make_async_copy(q_hbm, q_buf, q_sem).wait()
    steps = 2 * heads
    chip = [k - c, k - c + 1]

    @pl.loop(0, heads)
    def _(h):
        @pl.when(h == heads - 1)
        def _():
            relay(0, 0)

        @pl.when(c == 1)
        def _():
            arrived(k_core, h, 0)
            arrived(k_core, h, 1)

        @pl.when(h == 0)
        def _():
            build_ext(k_core, True)

        weigh(chip, h, True)
        add_up(chip, h, True, False)

    @pl.loop(0, steps)
    def _(step):
        phase = step // heads
        h = lax.rem(step, heads)
        z_level = 1 + phase
        x_level = z_level - x
        slot_list = [
            (x_level if spot < 2 else z_level) * PLANE + spot for spot in range(PLANE)
        ]

        relay(step, 1)
        from_core(step, 0)

        @pl.when(h == 0)
        def _():
            for spot, slot in enumerate(slot_list):
                build_ext(slot, z >= (x_level if spot < 2 else z_level))

        @pl.when(z >= x_level)
        def _():
            weigh(slot_list, h, False)

        @pl.when(step + 1 < steps)
        def _():
            relay(step + 1, 0)

        from_core(step, 1)

        @pl.when((phase == 0) & (z >= x_level))
        def _():
            add_up(slot_list, h, False, False)

        @pl.when((phase == 1) & (z >= x_level))
        def _():
            add_up(slot_list, h, False, True)

        @pl.when((phase == 1) & (z < x_level))
        def _():
            @pl.loop(0, group)
            def _(g):
                done = acc[h, g]
                o_buf[:, columns(h, g)] = (done[:, :HD] / done[:, HD:]).astype(jnp.bfloat16)

    for copy in page_copies():
        copy.wait()

    @pl.when(has_up)
    def _():
        all_sent(k, z_sem.at[0])

    @pl.when(has_up & (z >= 1))
    def _():
        all_sent(PLANE + k, z_sem.at[1])

    @pl.when(has_up & (z >= 1) & (x == 0))
    def _():
        side_send().wait_send()

    @pl.when(x == 0)
    def _():
        all_sent(k, x_sem.at[0])

    @pl.when(z >= 1)
    def _():
        all_sent(PLANE + k, x_sem.at[1])

    @pl.when((z >= 2) & (x == 1))
    def _():
        all_sent(2 * PLANE + k, x_sem.at[2], rows)

    @pl.when(c == 0)
    def _():
        all_sent(k, c_sem.at[k])

    for phase in range(2):
        level = 1 + phase

        @pl.when(z >= level)
        def _():
            all_sent(level * PLANE + k, c_sem.at[level * PLANE + k])

        @pl.when(z >= level - x)
        def _():
            slot = (level - x) * PLANE + k_x
            all_sent(slot, c_sem.at[slot])


def place_kernel(slots_ref, flat, context, context_hbm, cache_hbm, sems, context_sem):
    count = flat.shape[0]
    base = lax.axis_index("seq") * count
    whole = pltpu.make_async_copy(context, context_hbm, context_sem)
    whole.start()

    def copy(p):
        return pltpu.make_async_copy(
            flat.at[p], cache_hbm.at[slots_ref[p] - base], sems
        )

    for p in range(count):
        copy(p).start()
    pltpu.make_async_copy(flat, cache_hbm, sems).wait()
    whole.wait()


def in_hbm(array):
    return pltpu.with_memory_space_constraint(array, pltpu.HBM)


def local(n, queries, keys, values, segment_ids, page_slots):
    rows = queries.shape[0]
    heads = keys.shape[1] // HD
    group = queries.shape[1] // HD // heads
    page_dev = page_slots.shape[0]
    page = rows // page_dev
    any_spec = pl.BlockSpec(memory_space=pl.ANY)
    hbm_spec = pl.BlockSpec(memory_space=pltpu.HBM)
    vmem_spec = pl.BlockSpec(memory_space=pltpu.VMEM)
    slots = LEVELS * PLANE
    context_type = jax.ShapeDtypeStruct(queries.shape, jnp.bfloat16)
    cache_type = jax.ShapeDtypeStruct((page_dev, page // 2, 4 * heads * HD), jnp.bfloat16)
    context, flat = pl.pallas_call(
        functools.partial(kernel, n, heads, group),
        out_shape=(context_type, cache_type),
        in_specs=[hbm_spec] * 6,
        out_specs=(vmem_spec, vmem_spec),
        scratch_shapes=[
            pltpu.VMEM(queries.shape, jnp.bfloat16),
            pltpu.VMEM((slots, SEG_ROWS + heads * 2 * rows, HD), jnp.bfloat16),
            pltpu.VMEM((rows // HD, HD), jnp.int32),
            pltpu.VMEM((slots, rows, HD), jnp.bfloat16),
            pltpu.VMEM((rows, HD), jnp.bfloat16),
            pltpu.VMEM((heads, group, rows, 1), jnp.float32),
            pltpu.VMEM((group, rows, 1), jnp.float32),
            pltpu.VMEM((group, rows, PLANE * rows), jnp.bfloat16),
            pltpu.VMEM((heads, group, rows, 2 * HD), jnp.float32),
            pltpu.SemaphoreType.DMA,
            pltpu.SemaphoreType.DMA,
            pltpu.SemaphoreType.DMA,
            pltpu.SemaphoreType.DMA((2,)),
            pltpu.SemaphoreType.DMA((2,)),
            pltpu.SemaphoreType.DMA((2,)),
            pltpu.SemaphoreType.DMA((slots, heads, 2)),
            pltpu.SemaphoreType.DMA((LEVELS,)),
            pltpu.SemaphoreType.DMA((LEVELS,)),
            pltpu.SemaphoreType.DMA((slots,)),
        ],
        compiler_params=pltpu.CompilerParams(
            collective_id=0, has_side_effects=True, vmem_limit_bytes=36 * 2**20
        ),
    )(
        in_hbm(queries),
        in_hbm(keys),
        in_hbm(values),
        in_hbm(keys.reshape(page_dev, page, heads * HD)),
        in_hbm(values.reshape(page_dev, page, heads * HD)),
        in_hbm(segment_ids.reshape(rows // HD, HD)),
    )
    return pl.pallas_call(
        place_kernel,
        out_shape=(context_type, cache_type),
        in_specs=[pl.BlockSpec(memory_space=pltpu.SMEM), vmem_spec, vmem_spec],
        out_specs=(any_spec, any_spec),
        scratch_shapes=[pltpu.SemaphoreType.DMA, pltpu.SemaphoreType.DMA],
        compiler_params=pltpu.CompilerParams(vmem_limit_bytes=8 * 2**20),
    )(page_slots, flat, context)


def solution(mesh):
    placed = (P("seq", "mp"), P("seq", "mp"), P("seq", "mp"), P("seq"), P("seq"))
    return jax.shard_map(
        functools.partial(local, mesh.shape["seq"]),
        mesh=mesh,
        in_specs=placed,
        out_specs=(P("seq", "mp"), P("seq", "mp", None)),
        check_vma=False,
    )
```

```python
import functools
import math

import jax
import jax.numpy as jnp
from jax import lax
from jax.experimental import pallas as pl
from jax.experimental.pallas import tpu as pltpu
from jax.sharding import PartitionSpec as P

HD = 128
LMAX = 2048
PLANE = 4
LEVELS = 3
BIG = 2.0**30
HEAD = 2
SEG_ROWS = 16
EXP_SCALE = math.log2(math.e) / math.sqrt(HD)
NT = (((1,), (1,)), ((), ()))
NN = (((1,), (0,)), ((), ()))


def kernel(
    n,
    heads,
    group,
    q_hbm,
    k_hbm,
    v_hbm,
    k_pages,
    v_pages,
    seg_hbm,
    o_buf,
    flat,
    q_buf,
    buf,
    seg_ref,
    ext,
    feat,
    top,
    fade,
    weights,
    acc,
    local_sem,
    q_sem,
    seg_sem,
    page_send,
    page_recv,
    page_local,
    recv_sem,
    z_sem,
    x_sem,
    c_sem,
):
    rows = q_buf.shape[0]
    planes = n // PLANE
    me = lax.axis_index("seq")
    side = lax.axis_index("mp")
    z = me // PLANE
    k = lax.rem(me, PLANE)
    x = k // 2
    c = lax.rem(k, 2)
    k_core = k + 1 - 2 * c
    k_x = k_core + 2 - 4 * x
    k_diag = k + 2 - 4 * x
    core_dev = z * PLANE + k_core
    x_dev = z * PLANE + k_x
    up_dev = me + PLANE
    has_up = z + 1 < planes

    barrier = pltpu.get_barrier_semaphore()

    def greet(**where):
        pl.semaphore_signal(
            barrier, inc=1, device_id=where, device_id_type=pl.DeviceIdType.MESH
        )

    greet(seq=core_dev)
    greet(seq=x_dev)
    greet(mp=1 - side)

    @pl.when(has_up)
    def _():
        greet(seq=up_dev)

    @pl.when(z > 0)
    def _():
        greet(seq=me - PLANE)

    seg_copy = pltpu.make_async_copy(seg_hbm, seg_ref, seg_sem)
    seg_copy.start()

    def place(h, part):
        return pl.ds(pl.multiple_of(SEG_ROWS + (2 * h + part) * rows, SEG_ROWS), rows)

    @pl.loop(0, heads)
    def _(h):
        cols = pl.ds(pl.multiple_of(h * HD, HD), HD)
        for part, source in enumerate((k_hbm, v_hbm)):
            pltpu.make_async_copy(
                source.at[:, cols], buf.at[k, place(h, part)], local_sem
            ).start()

    pltpu.make_async_copy(q_hbm, q_buf, q_sem).start()
    seg_copy.wait()
    numbers = seg_ref[...].astype(jnp.float32)
    row = lax.broadcasted_iota(jnp.int32, (SEG_ROWS, HD), 0)
    spread = jnp.zeros((SEG_ROWS, HD), jnp.float32)
    for part in range(rows // HD):
        spread = jnp.where(row == part, numbers[part : part + 1, :], spread)
    buf[k, 0:SEG_ROWS] = spread.astype(jnp.bfloat16)
    loaded = buf.at[k, pl.ds(SEG_ROWS, heads * 2 * rows)]
    pltpu.make_async_copy(loaded, loaded, local_sem).wait()

    pl.semaphore_wait(
        barrier, 3 + jnp.where(has_up, 1, 0) + jnp.where(z > 0, 1, 0)
    )

    def send(source, slot, h, part, send_sem, device):
        if part == HEAD:
            where, part = pl.ds(0, SEG_ROWS + rows), 0
        else:
            where = place(h, part)
        return pltpu.make_async_remote_copy(
            src_ref=buf.at[source, where],
            dst_ref=buf.at[slot, where],
            send_sem=send_sem,
            recv_sem=recv_sem.at[slot, h, part],
            device_id={"seq": device},
            device_id_type=pl.DeviceIdType.MESH,
        )

    def up_send(level, h, part):
        source, slot = level * PLANE + k, (level + 1) * PLANE + k
        return send(source, slot, h, part, z_sem.at[level], up_dev)

    def x_send(level, h, part):
        return send(level * PLANE + k, level * PLANE + k, h, part, x_sem.at[level], x_dev)

    def core_send(slot, h, part):
        return send(slot, slot, h, part, c_sem.at[slot], core_dev)

    def all_sent(slot, send_sem):
        pltpu.make_async_remote_copy(
            src_ref=buf.at[slot],
            dst_ref=buf.at[slot],
            send_sem=send_sem,
            recv_sem=recv_sem.at[slot, 0, 0],
            device_id={"seq": core_dev},
            device_id_type=pl.DeviceIdType.MESH,
        ).wait_send()

    def piece(h, part, body):
        if part == 0:
            @pl.when(h == 0)
            def _():
                body(HEAD)

            @pl.when(h > 0)
            def _():
                body(0)
        else:
            body(1)

    def arrived(slot, h, part):
        piece(h, part, lambda p: core_send(slot, h, p).wait_recv())

    @pl.loop(0, heads)
    def _(h):
        def begin(part):
            @pl.when(has_up)
            def _():
                up_send(0, h, part).start()

            @pl.when(x == 0)
            def _():
                x_send(0, h, part).start()

            @pl.when(c == 0)
            def _():
                core_send(k, h, part).start()

        piece(h, 0, begin)
        piece(h, 1, begin)

    slots = flat.shape[1]
    width = heads * HD

    def page_copies():
        out = []
        for kv, pages in enumerate((k_pages, v_pages)):
            dst = flat.at[
                :, :, pl.ds(pl.multiple_of(kv * 2 * width + side * width, HD), width)
            ]
            away = pages.at[:, pl.ds(pl.multiple_of((1 - side) * slots, slots), slots), :]
            here = pages.at[:, pl.ds(pl.multiple_of(side * slots, slots), slots), :]
            out.append(
                pltpu.make_async_remote_copy(
                    src_ref=away,
                    dst_ref=dst,
                    send_sem=page_send.at[kv],
                    recv_sem=page_recv.at[kv],
                    device_id={"mp": 1 - side},
                    device_id_type=pl.DeviceIdType.MESH,
                )
            )
            out.append(pltpu.make_async_copy(here, dst, page_local.at[kv]))
        return out

    for copy in page_copies():
        copy.start()

    def clear(first, count=PLANE):
        @pl.loop(first, first + count)
        def _(slot):
            buf[slot, 0:SEG_ROWS] = jnp.zeros((SEG_ROWS, HD), buf.dtype)

            @pl.loop(0, 2 * heads)
            def _(half):
                buf[slot, place(0, half)] = jnp.zeros((rows, HD), buf.dtype)

    @pl.when(c == 0)
    def _():
        clear(k_core, 1)

    @pl.when(z < 1)
    def _():
        clear(PLANE)

    @pl.when(z < 2)
    def _():
        clear(2 * PLANE)

    def build_ext(slot, present):
        seg = buf[slot, 0:SEG_ROWS].astype(jnp.float32)
        other = jnp.where(present, 0.0, 1.0)
        number = lax.broadcasted_iota(jnp.int32, (HD, HD), 0).astype(jnp.float32)
        for part in range(rows // HD):
            hot = jnp.where(number == seg[part : part + 1, :], 1.0, other)
            ext[slot, part * HD : (part + 1) * HD, :] = hot.T.astype(jnp.bfloat16)

    build_ext(k, True)
    feat[...] = ((ext[k].astype(jnp.float32) - 1.0) * BIG).astype(jnp.bfloat16)
    ones = jnp.ones((rows, HD), jnp.bfloat16)

    def columns(h, g):
        return pl.ds(pl.multiple_of((h * group + g) * HD, HD), HD)

    def weigh(slot_list, h, first):
        width = len(slot_list) * rows
        keys = jnp.concatenate(
            [jnp.concatenate([buf[s, place(h, 0)], ext[s]], axis=1) for s in slot_list],
            axis=0,
        )

        def scores(g):
            query = jnp.concatenate([q_buf[:, columns(h, g)], feat[...]], axis=1)
            return lax.dot_general(query, keys, NT, preferred_element_type=jnp.float32)

        following = scores(0)
        for g in range(group):
            score = following
            if g + 1 < group:
                following = scores(g + 1)
            if first:
                later = lax.broadcasted_iota(jnp.int32, score.shape, 1) > (
                    lax.broadcasted_iota(jnp.int32, score.shape, 0) + c * rows
                )
                score = jnp.where(later, -BIG, score)
            best = jnp.max(score, axis=1, keepdims=True)
            if not first:
                old = top[h, g]
                best = jnp.maximum(old, best)
                fade[g] = jnp.exp2((old - best) * EXP_SCALE)
            top[h, g] = best
            weight = jnp.exp2((score - best) * EXP_SCALE).astype(jnp.bfloat16)
            weights[g, :, 0:width] = weight

    def add_up(slot_list, h, first, last):
        width = len(slot_list) * rows
        vals = jnp.concatenate(
            [jnp.concatenate([buf[s, place(h, 1)], ones], axis=1) for s in slot_list],
            axis=0,
        )
        for g in range(group):
            new = lax.dot_general(
                weights[g, :, 0:width], vals, NN, preferred_element_type=jnp.float32
            )
            if not first:
                new = new + acc[h, g] * fade[g]
            if last:
                o_buf[:, columns(h, g)] = (new[:, :HD] / new[:, HD:]).astype(jnp.bfloat16)
            else:
                acc[h, g] = new

    def relay(step, part):
        phase = step // heads
        h = lax.rem(step, heads)
        z_level = 1 + phase
        x_level = z_level - x

        @pl.when(z >= z_level)
        def _():
            slot = z_level * PLANE + k

            def pass_on(p):
                core_send(slot, h, p).wait_recv()

                @pl.when((x == 1) | (phase == 0))
                def _():
                    x_send(z_level, h, p).start()

                core_send(slot, h, p).start()

                @pl.when((phase == 0) & has_up)
                def _():
                    up_send(1, h, p).start()

            piece(h, part, pass_on)

        @pl.when(z >= x_level)
        def _():
            slot = x_level * PLANE + k_x

            def pass_on(p):
                core_send(slot, h, p).wait_recv()
                core_send(slot, h, p).start()

            piece(h, part, pass_on)

    def from_core(step, part):
        phase = step // heads
        h = lax.rem(step, heads)
        z_level = 1 + phase
        x_level = z_level - x

        @pl.when(z >= z_level)
        def _():
            arrived(z_level * PLANE + k_core, h, part)

        @pl.when(z >= x_level)
        def _():
            arrived(x_level * PLANE + k_diag, h, part)

    pltpu.make_async_copy(q_hbm, q_buf, q_sem).wait()
    steps = 2 * heads
    chip = [k - c, k - c + 1]

    @pl.loop(0, heads)
    def _(h):
        @pl.when(h == heads - 1)
        def _():
            relay(0, 0)

        @pl.when(c == 1)
        def _():
            arrived(k_core, h, 0)
            arrived(k_core, h, 1)

        @pl.when(h == 0)
        def _():
            build_ext(k_core, True)

        weigh(chip, h, True)
        add_up(chip, h, True, False)

    @pl.loop(0, steps)
    def _(step):
        phase = step // heads
        h = lax.rem(step, heads)
        z_level = 1 + phase
        x_level = z_level - x
        slot_list = [
            (x_level if spot < 2 else z_level) * PLANE + spot for spot in range(PLANE)
        ]

        relay(step, 1)
        from_core(step, 0)

        @pl.when(h == 0)
        def _():
            for spot, slot in enumerate(slot_list):
                build_ext(slot, z >= (x_level if spot < 2 else z_level))

        weigh(slot_list, h, False)

        @pl.when(step + 1 < steps)
        def _():
            relay(step + 1, 0)

        from_core(step, 1)

        @pl.when(phase == 0)
        def _():
            add_up(slot_list, h, False, False)

        @pl.when(phase == 1)
        def _():
            add_up(slot_list, h, False, True)

    for copy in page_copies():
        copy.wait()

    @pl.when(has_up)
    def _():
        all_sent(k, z_sem.at[0])

    @pl.when(has_up & (z >= 1))
    def _():
        all_sent(PLANE + k, z_sem.at[1])

    @pl.when(x == 0)
    def _():
        all_sent(k, x_sem.at[0])

    @pl.when(z >= 1)
    def _():
        all_sent(PLANE + k, x_sem.at[1])

    @pl.when((z >= 2) & (x == 1))
    def _():
        all_sent(2 * PLANE + k, x_sem.at[2])

    @pl.when(c == 0)
    def _():
        all_sent(k, c_sem.at[k])

    for phase in range(2):
        level = 1 + phase

        @pl.when(z >= level)
        def _():
            all_sent(level * PLANE + k, c_sem.at[level * PLANE + k])

        @pl.when(z >= level - x)
        def _():
            slot = (level - x) * PLANE + k_x
            all_sent(slot, c_sem.at[slot])


def place_kernel(slots_ref, flat, context, context_hbm, cache_hbm, sems, context_sem):
    count = flat.shape[0]
    base = lax.axis_index("seq") * count
    whole = pltpu.make_async_copy(context, context_hbm, context_sem)
    part = context.shape[0] // 4
    for i in range(4):
        some = pl.ds(i * part, part)
        pltpu.make_async_copy(context.at[some], context_hbm.at[some], context_sem).start()

    def copy(p):
        return pltpu.make_async_copy(
            flat.at[p], cache_hbm.at[slots_ref[p] - base], sems
        )

    for p in range(count):
        copy(p).start()
    pltpu.make_async_copy(flat, cache_hbm, sems).wait()
    whole.wait()


def in_hbm(array):
    return pltpu.with_memory_space_constraint(array, pltpu.HBM)


def local(n, queries, keys, values, segment_ids, page_slots):
    rows = queries.shape[0]
    heads = keys.shape[1] // HD
    group = queries.shape[1] // HD // heads
    page_dev = page_slots.shape[0]
    page = rows // page_dev
    any_spec = pl.BlockSpec(memory_space=pl.ANY)
    hbm_spec = pl.BlockSpec(memory_space=pltpu.HBM)
    vmem_spec = pl.BlockSpec(memory_space=pltpu.VMEM)
    slots = LEVELS * PLANE
    context_type = jax.ShapeDtypeStruct(queries.shape, jnp.bfloat16)
    cache_type = jax.ShapeDtypeStruct((page_dev, page // 2, 4 * heads * HD), jnp.bfloat16)
    context, flat = pl.pallas_call(
        functools.partial(kernel, n, heads, group),
        out_shape=(context_type, cache_type),
        in_specs=[hbm_spec] * 6,
        out_specs=(vmem_spec, vmem_spec),
        scratch_shapes=[
            pltpu.VMEM(queries.shape, jnp.bfloat16),
            pltpu.VMEM((slots, SEG_ROWS + heads * 2 * rows, HD), jnp.bfloat16),
            pltpu.VMEM((rows // HD, HD), jnp.int32),
            pltpu.VMEM((slots, rows, HD), jnp.bfloat16),
            pltpu.VMEM((rows, HD), jnp.bfloat16),
            pltpu.VMEM((heads, group, rows, 1), jnp.float32),
            pltpu.VMEM((group, rows, 1), jnp.float32),
            pltpu.VMEM((group, rows, PLANE * rows), jnp.bfloat16),
            pltpu.VMEM((heads, group, rows, 2 * HD), jnp.float32),
            pltpu.SemaphoreType.DMA,
            pltpu.SemaphoreType.DMA,
            pltpu.SemaphoreType.DMA,
            pltpu.SemaphoreType.DMA((2,)),
            pltpu.SemaphoreType.DMA((2,)),
            pltpu.SemaphoreType.DMA((2,)),
            pltpu.SemaphoreType.DMA((slots, heads, 2)),
            pltpu.SemaphoreType.DMA((LEVELS,)),
            pltpu.SemaphoreType.DMA((LEVELS,)),
            pltpu.SemaphoreType.DMA((slots,)),
        ],
        compiler_params=pltpu.CompilerParams(
            collective_id=0, has_side_effects=True, vmem_limit_bytes=36 * 2**20
        ),
    )(
        in_hbm(queries),
        in_hbm(keys),
        in_hbm(values),
        in_hbm(keys.reshape(page_dev, page, heads * HD)),
        in_hbm(values.reshape(page_dev, page, heads * HD)),
        in_hbm(segment_ids.reshape(rows // HD, HD)),
    )
    return pl.pallas_call(
        place_kernel,
        out_shape=(context_type, cache_type),
        in_specs=[pl.BlockSpec(memory_space=pltpu.SMEM), vmem_spec, vmem_spec],
        out_specs=(any_spec, any_spec),
        scratch_shapes=[pltpu.SemaphoreType.DMA, pltpu.SemaphoreType.DMA],
        compiler_params=pltpu.CompilerParams(vmem_limit_bytes=8 * 2**20),
    )(page_slots, flat, context)


def solution(mesh):
    placed = (P("seq", "mp"), P("seq", "mp"), P("seq", "mp"), P("seq"), P("seq"))
    return jax.shard_map(
        functools.partial(local, mesh.shape["seq"]),
        mesh=mesh,
        in_specs=placed,
        out_specs=(P("seq", "mp"), P("seq", "mp", None)),
        check_vma=False,
    )
```
